32 devices in a mesh: dp: 4 (over y, core), fsdp: 8 (over z, x).
Axes of the slice: x: 2, y: 2, z: 4, core: 2. Of those that a mesh axis runs over, the one named last changes fastest.
Arguments:
- inputs: bfloat16 [128, 256, 768], P(('dp', 'fsdp')), may hold values from -6 to 6
- dealing: int32 [128], replicated, may hold values from 0 to 127, as said below
- lengths: int32 [128], replicated, may hold values from 32 to 256, as said below
- proj_qkv: bfloat16 [3, 768, 768], P(None, ('dp', 'fsdp')), may hold values from -0.3125 to 0.3125
- bias_qv: bfloat16 [2, 768], P(None, ('dp', 'fsdp')), may hold values from -1 to 1
- proj_out: bfloat16 [768, 768], P(('dp', 'fsdp')), may hold values from -1.5 to 1.5
- bias_out: bfloat16 [768], P(('dp', 'fsdp')), may hold values from -1.5 to 1.5
- gain_one: bfloat16 [768], P(('dp', 'fsdp')), may hold values from 0.5 to 1.5
- offset_one: bfloat16 [768], P(('dp', 'fsdp')), may hold values from -1 to 1
- proj_up: bfloat16 [768, 3072], P(('dp', 'fsdp')), may hold values from -0.21875 to 0.21875
- bias_up: bfloat16 [3072], P(('dp', 'fsdp')), may hold values from -1.5 to 1.5
- proj_down: bfloat16 [3072, 768], P(('dp', 'fsdp')), may hold values from -0.109375 to 0.109375
- bias_down: bfloat16 [768], P(('dp', 'fsdp')), may hold values from -1 to 1
- gain_two: bfloat16 [768], P(('dp', 'fsdp')), may hold values from 0.5 to 1.5
- offset_two: bfloat16 [768], P(('dp', 'fsdp')), may hold values from -1 to 1
- cotangent: bfloat16 [128, 256, 768], P(('dp', 'fsdp')), may hold values from -6 to 6
Outputs:
- layer_out: bfloat16 [128, 256, 768], P(('dp', 'fsdp'))
- input_grad: bfloat16 [128, 256, 768], P(('dp', 'fsdp'))
- grad_proj_qkv: float32 [3, 768, 768], P(None, ('dp', 'fsdp'))
- grad_bias_qv: float32 [2, 768], P(None, ('dp', 'fsdp'))
- grad_proj_out: float32 [768, 768], P(('dp', 'fsdp'))
- grad_bias_out: float32 [768], P(('dp', 'fsdp'))
- grad_gain_one: float32 [768], P(('dp', 'fsdp'))
- grad_offset_one: float32 [768], P(('dp', 'fsdp'))
- grad_proj_up: float32 [768, 3072], P(('dp', 'fsdp'))
- grad_bias_up: float32 [3072], P(('dp', 'fsdp'))
- grad_proj_down: float32 [3072, 768], P(('dp', 'fsdp'))
- grad_bias_down: float32 [768], P(('dp', 'fsdp'))
- grad_gain_two: float32 [768], P(('dp', 'fsdp'))
- grad_offset_two: float32 [768], P(('dp', 'fsdp'))
The draws below stay inside these ranges and needn't reach their ends.
Inputs may be any that keep to these rules, and one draw needn't show every extreme that they name: dealing is a permutation of the sequences. With device g = dp index * 8 + fsdp index holding sequences and dealt positions g * 4 to g * 4 + 3, every sequence is dealt to a device of the same fsdp index; a device's 4 dealt positions come from 4 different devices, and a device's 4 sequences go to 4 different devices. `lengths`: key positions at or beyond a sequence's length are padding.
All inputs are finite; a program needn't handle non-finite values.
Results may differ from the reference program's by a relative error of at most 0.015.
The reference program's roundings to bfloat16 on the way count: a program that leaves them out, or rounds other values in their place, can miss the bound.
Values may be sent and summed in bfloat16 or wider, within the bound.
No kernel may reach another device: no remote copies, remote signals or barrier semaphores. Data moves between devices by JAX's collectives and lax.ppermute only.
A program may use at most 192 MiB of HBM per device.

```python
import jax
import jax.numpy as jnp
from jax import lax

D = 768
H = 12
HD = 64
FF = 3072
L = 256
SEQ_DEV = 4
SEQS = 128
N_DP = 4
N_FSDP = 8


def draw_lengths(key, part):
    base_key = jax.random.fold_in(key, 31)
    drawn = jax.random.randint(base_key, (SEQS,), L // 8, L + 1, dtype=jnp.int32)
    position = jnp.arange(SEQS, dtype=jnp.int32) % 16
    drawn = jnp.where(position == 0, L, drawn)
    drawn = jnp.where(position == 1, L // 8, drawn)
    return drawn.astype(jnp.int32)


def deal_group(group_key, column):
    key_order, key_shift, key_slots = jax.random.split(group_key, 3)
    order_dp = jax.random.permutation(key_order, N_DP).astype(jnp.int32)
    place_dp = jnp.zeros((N_DP,), jnp.int32).at[order_dp].set(jnp.arange(N_DP, dtype=jnp.int32))
    shifts = jax.random.permutation(key_shift, N_DP).astype(jnp.int32)[:SEQ_DEV]
    slot_orders = jax.vmap(lambda sub_key: jax.random.permutation(sub_key, SEQ_DEV).astype(jnp.int32))(jax.random.split(key_slots, N_DP))
    receiver = jnp.arange(N_DP, dtype=jnp.int32)[:, None]
    sender = order_dp[(place_dp[receiver] + shifts[None, :]) % N_DP]
    sender_slot = slot_orders[sender, jnp.arange(SEQ_DEV, dtype=jnp.int32)[None, :]]
    return (sender * N_FSDP + column) * SEQ_DEV + sender_slot


def draw_dealing(key, part):
    base_key = jax.random.fold_in(key, 17)
    group_keys = jax.random.split(base_key, N_FSDP)
    table = jax.vmap(deal_group)(group_keys, jnp.arange(N_FSDP, dtype=jnp.int32))
    return jnp.transpose(table, (1, 0, 2)).reshape(SEQS).astype(jnp.int32)


def raised(values, key, source, target, shards_of, factor):
    def block_of(dim):
        return (jnp.arange(values.shape[dim]) // (values.shape[dim] // shards_of)).reshape((-1,) + (1,) * (values.ndim - 1 - dim))

    one_side = jax.random.permutation(key, shards_of)[block_of(target)]
    second = (block_of(target) + shards_of // 2) % shards_of
    return jnp.where((block_of(source) == one_side) | (block_of(source) == second), factor * values, values)


def block_levels(own_key, shape, pieces, least, top_value):
    factor_of = 1.0
    for dim, shards_of in pieces:
        heights = jax.random.uniform(jax.random.fold_in(jax.random.fold_in(own_key, 6), dim), (shards_of,), jnp.float32, least / len(pieces), top_value / len(pieces))
        factor_of = factor_of * jnp.repeat(jnp.exp(heights), shape[dim] // shards_of).reshape((-1,) + (1,) * (len(shape) - 1 - dim))
    return factor_of


def centred(key, dims, deviation, limit, shards=(), held_as=jnp.bfloat16):
    values = jax.random.normal(key, dims, jnp.float32) * deviation
    if len(shards) > 0:
        values = block_levels(key, dims, shards, -0.22, 0.18) * values
    return jnp.clip(values, min=-limit, max=limit).astype(held_as)


def bell_draw_with(key, extent, spread, limit, cuts, heavy, kind=jnp.bfloat16):
    entries = spread * jax.random.normal(key, extent, jnp.float32)
    if cuts:
        entries = entries * block_levels(key, extent, cuts, -0.22, 0.18)
    return jnp.clip(raised(entries, jax.random.fold_in(key, 3), *heavy), -limit, limit).astype(kind)


def setup_inputs(seed: int = 0) -> dict:
    key_of = jax.random.split(jax.random.key(seed), 17)
    return {
        "inputs": bell_draw_with(key_of[0], (SEQS, L, D), 1.0, 6.0, ((0, 32),), (0, 2, 32, 2.75)),
        "dealing": draw_dealing(jax.random.fold_in(key_of[16], 71), 0),
        "lengths": draw_lengths(jax.random.fold_in(key_of[16], 71), 0),
        "proj_qkv": centred(key_of[3], (3, D, D), (D // 2) ** -0.5, 0.3125, ((1, 32),)),
        "bias_qv": centred(key_of[4], (2, D), 0.2, 1.0, ((1, 32),)),
        "proj_out": centred(key_of[5], (D, D), (D // 48) ** -0.5, 1.5, ((0, 32),)),
        "bias_out": centred(key_of[6], (D,), 0.3, 1.5, ((0, 32),)),
        "gain_one": jnp.clip(1.0 + 0.1 * jax.random.normal(key_of[7], (D,), jnp.float32), 0.5, 1.5).astype(jnp.bfloat16),
        "offset_one": centred(key_of[8], (D,), 0.2, 1.0, ((0, 32),)),
        "proj_up": centred(key_of[9], (D, FF), D ** -0.5, 0.21875, ((0, 32),)),
        "bias_up": centred(key_of[10], (FF,), 0.3, 1.5, ((0, 32),)),
        "proj_down": centred(key_of[11], (FF, D), FF ** -0.5, 0.109375, ((0, 32),)),
        "bias_down": centred(key_of[12], (D,), 0.2, 1.0, ((0, 32),)),
        "gain_two": jnp.clip(1.0 + 0.1 * jax.random.normal(key_of[13], (D,), jnp.float32), 0.5, 1.5).astype(jnp.bfloat16),
        "offset_two": centred(key_of[14], (D,), 0.2, 1.0, ((0, 32),)),
        "cotangent": bell_draw_with(key_of[15], (SEQS, L, D), 1.0, 6.0, ((0, 32),), (0, 2, 32, 2.75)),
    }


EPS = 1e-12
SCALE = 0.125
HIGH = lax.Precision.HIGHEST

@jax.custom_vjp
def low(v):
    return lax.optimization_barrier(v.astype(jnp.bfloat16)).astype(jnp.float32)

@jax.custom_vjp
def low_back(v):
    return v

def low_keep(v):
    return (low(v), None)

def low_pass(kept, grad):
    return (grad,)

def back_keep(v):
    return (v, None)

def back_low(kept, grad):
    return (low(grad),)
low.defvjp(low_keep, low_pass)
low_back.defvjp(back_keep, back_low)

def rounded(value):
    return low_back(low(value))

def layer_norm(hidden, norm_gain, norm_offset):
    center = hidden - lax.optimization_barrier(jnp.mean(hidden, axis=-1, keepdims=True))
    normed = center * lax.rsqrt(lax.optimization_barrier(jnp.mean(center * center, axis=-1, keepdims=True)) + EPS)
    return normed * norm_gain + norm_offset

def layer(seq_in, seq_lens, weight_list):
    proj_qkv, bias_qv, proj_out, bias_out, gain_one, offset_one, proj_up, bias_up, proj_down, bias_down, gain_two, offset_two = weight_list
    groups, length, model_width = seq_in.shape
    flat_in = seq_in.reshape(groups * length, model_width)
    queries = rounded(jnp.dot(flat_in, proj_qkv[0], precision=HIGH) + bias_qv[0]).reshape(groups, length, H, HD)
    key_rows = rounded(jnp.dot(flat_in, proj_qkv[1], precision=HIGH)).reshape(groups, length, H, HD)
    values = rounded(jnp.dot(flat_in, proj_qkv[2], precision=HIGH) + bias_qv[1]).reshape(groups, length, H, HD)
    live_keys = (jnp.arange(length)[None, :] < seq_lens[:, None])[:, None, None, :]
    scores = low_back(jnp.einsum('gqhd,gkhd->ghqk', queries, key_rows, precision=HIGH) * SCALE)
    scores = jnp.where(live_keys, scores, -1000000000.0)
    shifted = jnp.exp(scores - lax.optimization_barrier(jnp.max(scores, axis=-1, keepdims=True)))
    attn_probs = shifted / lax.optimization_barrier(jnp.sum(shifted, axis=-1, keepdims=True))
    context = rounded(jnp.einsum('ghqk,gkhd->gqhd', low(attn_probs), values, precision=HIGH))
    context = context.reshape(groups * length, model_width)
    attn_out = low_back(jnp.dot(context, proj_out, precision=HIGH) + bias_out)
    normed_mid = layer_norm(flat_in + attn_out, gain_one, offset_one)
    up_value = low_back(jnp.dot(low(normed_mid), proj_up, precision=HIGH) + bias_up)
    hidden = low(jax.nn.gelu(up_value, approximate=False))
    ffn_out = low_back(jnp.dot(hidden, proj_down, precision=HIGH) + bias_down)
    return layer_norm(normed_mid + ffn_out, gain_two, offset_two).reshape(groups, length, model_width)

def reference(inputs, dealing, lengths, proj_qkv, bias_qv, proj_out, bias_out, gain_one, offset_one, proj_up, bias_up, proj_down, bias_down, gain_two, offset_two, cotangent):
    weight_list = tuple((w.astype(jnp.float32) for w in (proj_qkv, bias_qv, proj_out, bias_out, gain_one, offset_one, proj_up, bias_up, proj_down, bias_down, gain_two, offset_two)))
    seq_total, length, model_width = inputs.shape
    group_count = seq_total // SEQ_DEV
    dealt_in = inputs[dealing].astype(jnp.float32).reshape(group_count, SEQ_DEV, length, model_width)
    dealt_len = lengths[dealing].reshape(group_count, SEQ_DEV)
    dealt_cot = cotangent.astype(jnp.float32).reshape(group_count, SEQ_DEV, length, model_width)

    def one_group(running, group_item):
        group_in, group_len, group_cot = group_item

        def forward(seq_x, *params_in):
            return layer(seq_x, group_len, params_in)
        group_out, pullback = jax.vjp(forward, group_in, *weight_list)
        grad_parts = pullback(group_cot)
        running = tuple((acc + part for acc, part in zip(running, grad_parts[1:])))
        return (running, (group_out.astype(jnp.bfloat16), grad_parts[0].astype(jnp.bfloat16)))
    start = tuple((jnp.zeros_like(w) for w in weight_list))
    totals, (dealt_out, dealt_grad) = lax.scan(one_group, start, (dealt_in, dealt_len, dealt_cot))
    layer_out = dealt_out.reshape(seq_total, length, model_width)
    flat_grad = dealt_grad.reshape(seq_total, length, model_width)
    input_grad = jnp.zeros_like(flat_grad).at[dealing].set(flat_grad)
    return (layer_out, input_grad, totals[0], totals[1], totals[2], totals[3], totals[4], totals[5], totals[6], totals[7], totals[8], totals[9], totals[10], totals[11])
```

```python
import jax
import jax.numpy as jnp
from jax import lax
from jax.experimental import pallas as pl
from jax.experimental.pallas import tpu as pltpu
from jax.sharding import PartitionSpec as P

H = 12
HD = 64
AXES = ("dp", "fsdp")
NZ = 4

EPS = 1e-12
SCALE = 0.125
BF = jnp.bfloat16
F32 = jnp.float32


class Grid:
    def __init__(self, dp, fsdp):
        self.fsdp = fsdp
        self.size = {"y": dp // 2, "c": 2, "z": NZ, "x": fsdp // NZ}

    def flat(self, q):
        return (q["y"] * 2 + q["c"]) * self.fsdp + q["z"] * self.size["x"] + q["x"]

    def pairs(self, axis, step):
        result = []
        for y in range(self.size["y"]):
            for c in range(2):
                for z in range(NZ):
                    for x in range(self.size["x"]):
                        q = dict(y=y, c=c, z=z, x=x)
                        t = dict(q)
                        t[axis] = (q[axis] + step) % self.size[axis]
                        result.append((self.flat(q), self.flat(t)))
        return result

    def move(self, array, axis, step):
        return lax.ppermute(array, AXES, self.pairs(axis, step))

    def moved(self, bundle, axis, step):
        labels = []
        for mat, rel, rows in bundle[1]:
            rel = dict(rel)
            rel[axis] = (rel[axis] - step) % self.size[axis]
            labels.append((mat, rel, rows))
        return (self.move(bundle[0], axis, step), labels)


HERE = dict(y=0, c=0, z=0, x=0)


def rows_of(labels):
    return sum(rows for _, _, rows in labels)


def join(bundles):
    if len(bundles) == 1:
        return bundles[0]
    return (
        jnp.concatenate([b[0] for b in bundles], axis=0),
        [label for b in bundles for label in b[1]],
    )


def cut(bundle, count):
    array, labels = bundle
    at = rows_of(labels[:count])
    return (array[:at], labels[:count]), (array[at:], labels[count:])


def halves(bundle):
    labels = bundle[1]
    total = rows_of(labels)
    best = min(range(1, len(labels)), key=lambda i: abs(2 * rows_of(labels[:i]) - total))
    return cut(bundle, best)


def gather_axis(grid, bundle, axis):
    n = grid.size[axis]
    if n == 2:
        return [bundle, grid.moved(bundle, axis, 1)]
    up, down = grid.moved(bundle, axis, 1), grid.moved(bundle, axis, -1)
    got = [bundle, up, down]
    for _ in range(2, n // 2):
        up, down = grid.moved(up, axis, 1), grid.moved(down, axis, -1)
        got += [up, down]
    got += [
        grid.moved(halves(up)[0], axis, 1),
        grid.moved(halves(down)[1], axis, -1),
    ]
    return got


def gather_xy(grid, bundle):
    first, second = halves(bundle)
    first = join(gather_axis(grid, first, "x"))
    second = join(gather_axis(grid, second, "y"))
    return gather_axis(grid, first, "y") + gather_axis(grid, second, "x")


def gather_late_z(grid, bundle):
    return gather_axis(grid, join(gather_xy(grid, bundle)), "z")


def gather_early_z(grid, bundle):
    return gather_xy(grid, join(gather_axis(grid, bundle, "z")))


def gather_core(grid, bundles):
    return bundles + [grid.moved(b, "c", 1) for b in bundles]


def add_low(a, b):
    return (a.astype(F32) + b.astype(F32)).astype(BF)


def reduce_axis(grid, bundle, axis, wide=False):
    n = grid.size[axis]
    array, labels = bundle
    parts = []
    at = 0
    for r in range(n):
        mine = [label for label in labels if label[1][axis] == r]
        rows = rows_of(mine)
        parts.append((array[at : at + rows], mine))
        at += rows
    far = n // 2
    value = [p[0] for p in parts]
    if n > 2:
        low, high = halves(parts[far])
        split = low[0].shape[0]
        from_low = grid.move(low[0], axis, 1)
        from_high = grid.move(high[0], axis, -1)
        a, b = value[far - 1], value[n - far + 1]
        value[far - 1] = jnp.concatenate([add_low(a[:split], from_low), a[split:]], axis=0)
        value[n - far + 1] = jnp.concatenate([b[:split], add_low(b[split:], from_high)], axis=0)
        for k in range(far - 1, 1, -1):
            value[k - 1] = add_low(value[k - 1], grid.move(value[k], axis, 1))
            value[n - k + 1] = add_low(value[n - k + 1], grid.move(value[n - k], axis, -1))
    total = value[0].astype(F32) + grid.move(value[1], axis, 1).astype(F32)
    if n > 2:
        total = total + grid.move(value[n - 1], axis, -1).astype(F32)
    return (total if wide else total.astype(BF), parts[0][1])


def reduce_pair(grid, first, second, wide=False):
    first = reduce_axis(grid, reduce_axis(grid, first, "y"), "x", wide)
    second = reduce_axis(grid, reduce_axis(grid, second, "x"), "y", wide)
    return first, second


def order(axes, grid, mats):
    labels = [dict(HERE)]
    for axis in axes:
        labels = [dict(q, **{axis: r}) for q in labels for r in range(grid.size[axis])]
    return [(mat, q, rows) for q in labels for mat, rows in mats]


def late_z_labels(grid, first, second):
    near = order("yx", grid, first), order("xy", grid, second)
    result = []
    for c in range(2):
        labels = []
        for z in range(NZ):
            for part in near:
                labels += [(m, dict(q, z=z, c=c), rows) for m, q, rows in part]
        result.append(labels)
    return result


def early_z_labels(grid, axes, mats):
    return [
        [(m, dict(q, c=c), rows) for m, q, rows in order(axes + "z", grid, mats)]
        for c in range(2)
    ]


def reduce_late_z(grid, bundle, first_labels):
    first, second = cut(reduce_axis(grid, bundle, "z"), first_labels)
    return reduce_pair(grid, first, second, wide=True)


def reduce_early_z(grid, first, second):
    first, second = reduce_pair(grid, first, second)
    pieces = []
    for z in range(NZ):
        for array, labels in (first, second):
            before = rows_of([l for l in labels if l[1]["z"] < z])
            mine = [l for l in labels if l[1]["z"] == z]
            pieces.append((array[before : before + rows_of(mine)], mine))
    return reduce_axis(grid, join(pieces), "z", wide=True)


def add_core(grid, pair):
    (keep, labels), (send, _) = pair
    return (add_low(keep, grid.move(send, "c", 1)), labels)


def owner_of(grid, place, rel):
    q = {a: lax.rem(place[i] + rel[a], grid.size[a]) for i, a in enumerate("yczx")}
    return grid.flat(q)


def assemble(grid, place, bundles, targets, shapes):
    def body(place_ref, *refs):
        ins, outs, sems = refs[: len(bundles)], refs[len(bundles) : -1], refs[-1]
        here = [place_ref[i] for i in range(4)]
        for ref, (_, labels) in zip(ins, bundles):
            at = 0
            for mat, rel, rows in labels:
                which, base, column = targets[mat]
                start = pl.multiple_of(owner_of(grid, here, rel) * rows, 8) + base
                width = ref.shape[1]
                pltpu.make_async_copy(
                    ref.at[pl.ds(at, rows), :],
                    outs[which].at[pl.ds(start, rows), pl.ds(column, width)],
                    sems.at[which],
                ).start()
                at += rows
        for which, out in enumerate(outs):
            pltpu.make_async_copy(out, out, sems.at[which]).wait()

    return pl.pallas_call(
        body,
        out_shape=[jax.ShapeDtypeStruct(s, BF) for s in shapes],
        in_specs=[pl.BlockSpec(memory_space=pltpu.SMEM)]
        + [pl.BlockSpec(memory_space=pl.ANY)] * len(bundles),
        out_specs=[pl.BlockSpec(memory_space=pltpu.VMEM)] * len(shapes),
        scratch_shapes=[pltpu.SemaphoreType.DMA((len(shapes),))],
        compiler_params=pltpu.CompilerParams(vmem_limit_bytes=32 << 20),
    )(place, *[b[0] for b in bundles])


def spread(grid, place, matrices, sources, label_lists):
    width = min(m.shape[1] for m in matrices)

    def body(place_ref, *refs):
        ins = refs[: len(matrices)]
        outs = refs[len(matrices) : -1]
        sems = refs[-1]
        here = [place_ref[i] for i in range(4)]
        for k, (ref, labels) in enumerate(zip(outs, label_lists)):
            at = 0
            for mat, rel, rows in labels:
                which, column = sources[mat]
                start = pl.multiple_of(owner_of(grid, here, rel) * rows, 8)
                pltpu.make_async_copy(
                    ins[which].at[pl.ds(start, rows), pl.ds(column, width)],
                    ref.at[pl.ds(at, rows), :],
                    sems.at[k],
                ).start()
                at += rows
        for k, ref in enumerate(outs):
            pltpu.make_async_copy(ref, ref, sems.at[k]).wait()

    arrays = pl.pallas_call(
        body,
        out_shape=[jax.ShapeDtypeStruct((rows_of(l), width), BF) for l in label_lists],
        in_specs=[pl.BlockSpec(memory_space=pltpu.SMEM)]
        + [pl.BlockSpec(memory_space=pltpu.VMEM)] * len(matrices),
        out_specs=[pl.BlockSpec(memory_space=pl.ANY)] * len(label_lists),
        scratch_shapes=[pltpu.SemaphoreType.DMA((len(label_lists),))],
        compiler_params=pltpu.CompilerParams(vmem_limit_bytes=32 << 20),
    )(place, *matrices)
    return [(a, l) for a, l in zip(arrays, label_lists)]


TAIL = (
    0.16918961054406956,
    0.17069200193020534,
    0.14848198537671686,
    0.21443790550168065,
    -0.09363484535275278,
    0.5463999687025537,
    -0.5112305314832677,
    0.48509833626084115,
    -0.12943445092422354,
)


def dot(a,b): return jnp.dot(a,b,preferred_element_type=F32)
def dot_nt(a,b): return lax.dot_general(a,b,(((1,),(1,)),((),())),preferred_element_type=F32)

def gelu_parts(u):
    z = jnp.abs(u) * 0.7071067811865476
    t = 1.0 / (1.0 + 0.3 * z)
    q = jnp.full_like(t, TAIL[-1])
    for c in TAIL[-2::-1]:
        q = q * t + c
    e = jnp.exp(-(z * z))
    half = 0.5 * (e * t * q)
    return jnp.where(u < 0, half, 1.0 - half), e * 0.3989422804014327

def norm_stats(v):
    center = v - jnp.mean(v, axis=-1, keepdims=True)
    inverse = lax.rsqrt(jnp.mean(center * center, axis=-1, keepdims=True) + EPS)
    return center * inverse, inverse

def norm_back(grad, normed, inverse, gain):
    scaled = grad * gain
    return inverse * (scaled - jnp.mean(scaled, axis=-1, keepdims=True) - normed * jnp.mean(scaled * normed, axis=-1, keepdims=True))

def col_sum(v): return jnp.sum(v, axis=0, keepdims=True)

def middle(position, context, dealt, cot, vec, bias_up, w_out, w_up, w_down):
    n, length, width = dealt.shape
    ff = w_up.shape[1]
    chunks = ff // width
    def body(pos, ctx, x, g, vec, bu, wo, wu, wd, out, g_first, g_attn, hid, g_up, mid_low, g_ffn, sums, sum_up, slope):
        bias_out, gain_one, offset_one, bias_down, gain_two, offset_two = (vec[i:i+1] for i in range(2,8))
        first = x[0].astype(F32) + (dot(ctx[0], wo[...]) + bias_out)
        normed_one, inverse_one = norm_stats(first)
        mid = normed_one * gain_one + offset_one
        low = mid.astype(BF)
        mid_low[0] = low
        second = mid + bias_down
        for t in range(chunks):
            cols = slice(t*width,(t+1)*width)
            u = dot(low, wu[:, cols]) + bu[:, cols]
            phi, dens = gelu_parts(u)
            h = (u * phi).astype(BF)
            hid[0, :, cols] = h
            slope[:, cols] = phi + u * dens
            second += dot(h, wd[cols, :])
        normed_two, inverse_two = norm_stats(second)
        out[0] = (normed_two * gain_two + offset_two).astype(BF)
        gr = g[0].astype(F32)
        grad_second = norm_back(gr, normed_two, inverse_two, gain_two)
        low2 = grad_second.astype(BF)
        g_ffn[0] = low2
        @pl.when(pl.program_id(0) == 0)
        def _():
            sums[...] = jnp.zeros_like(sums)
            sum_up[...] = jnp.zeros_like(sum_up)
        grad_mid = grad_second
        for t in range(chunks):
            cols = slice(t*width,(t+1)*width)
            gu = (dot_nt(low2, wd[cols, :]) * slope[:, cols]).astype(BF)
            g_up[0, :, cols] = gu
            sum_up[:, cols] += col_sum(gu.astype(F32))
            grad_mid += dot_nt(gu, wu[:, cols])
        grad_first = norm_back(grad_mid, normed_one, inverse_one, gain_one)
        low3 = grad_first.astype(BF)
        g_first[0] = grad_first
        g_attn[0] = low3
        sums[2:3] += col_sum(low3.astype(F32))
        sums[3:4] += col_sum(grad_mid * normed_one)
        sums[4:5] += col_sum(grad_mid)
        sums[5:6] += col_sum(low2.astype(F32))
        sums[6:7] += col_sum(gr * normed_two)
        sums[7:8] += col_sum(gr)
    seq = lambda w: pl.BlockSpec((1, length, w), lambda i, pos: (i, 0, 0))
    dealt_seq = pl.BlockSpec((1, length, width), lambda i, pos: (pos[i], 0, 0))
    whole = lambda a: pl.BlockSpec(a.shape, lambda i, pos: (0,) * a.ndim, pipeline_mode=pl.Buffered(1))
    sh = lambda w, dt: jax.ShapeDtypeStruct((n, length, w), dt)
    acc = lambda r, w: pl.BlockSpec((r, w), lambda i, pos: (0, 0))
    return pl.pallas_call(
        body,
        out_shape=[sh(width,BF), sh(width,F32), sh(width,BF), sh(ff,BF), sh(ff,BF), sh(width,BF), sh(width,BF),
                   jax.ShapeDtypeStruct((8,width),F32), jax.ShapeDtypeStruct((1,ff),F32)],
        grid_spec=pltpu.PrefetchScalarGridSpec(num_scalar_prefetch=1, grid=(n,),
            in_specs=[seq(width), seq(width), dealt_seq, whole(vec), whole(bias_up), whole(w_out), whole(w_up), whole(w_down)],
            out_specs=[dealt_seq, seq(width), seq(width), seq(ff), seq(ff), seq(width), seq(width), acc(8,width), acc(1,ff)],
            scratch_shapes=[pltpu.VMEM((length, ff), F32)]),
        compiler_params=pltpu.CompilerParams(vmem_limit_bytes=60<<20),
    )(position, context, dealt, cot, vec, bias_up, w_out, w_up, w_down)

def halves_of(v, lane):
    zero = jnp.zeros_like(v)
    return jnp.where(lane, v, zero), jnp.where(lane, zero, v)

def attention_forward(lens, q, k, v):
    n, length, width = q.shape
    def body(lens, q, k, v, out):
        live = lax.broadcasted_iota(jnp.int32, (length, length), 0) < lens[pl.program_id(0)]
        lane = lax.broadcasted_iota(jnp.int32, (length, 128), 1) < HD
        for p in range(width // 128):
            cols = slice(p*128,(p+1)*128)
            q2, k2, v2 = q[0,:,cols], k[0,:,cols], v[0,:,cols]
            ka, kb = halves_of(k2, lane); va, vb = halves_of(v2, lane)
            acc = None
            for kh, vh in ((ka,va),(kb,vb)):
                s = jnp.where(live, dot_nt(kh, q2) * SCALE, -1000000000.0)
                e = jnp.exp(s - jnp.max(s, axis=0, keepdims=True))
                pr = (e / jnp.sum(e, axis=0, keepdims=True)).astype(BF)
                c = dot(vh.T, pr)
                acc = c if acc is None else acc + c
            out[0,:,cols] = acc.T.astype(BF)
    seq = pl.BlockSpec((1, length, width), lambda i, lens: (i, 0, 0))
    return pl.pallas_call(body, out_shape=jax.ShapeDtypeStruct(q.shape, BF),
        grid_spec=pltpu.PrefetchScalarGridSpec(num_scalar_prefetch=1, grid=(n,), in_specs=[seq]*3, out_specs=seq),
        compiler_params=pltpu.CompilerParams(vmem_limit_bytes=40<<20))(lens, q, k, v)

def attention_backward(lens, q, k, v, g_attn, g_first, w_out, w_qkv):
    n, length, width = q.shape
    def body(lens, q, k, v, ga, gf, wo, wqkv, dx, dq, dk, dv, sums):
        @pl.when(pl.program_id(0) == 0)
        def _(): sums[...] = jnp.zeros_like(sums)
        live = lax.broadcasted_iota(jnp.int32, (length, length), 0) < lens[pl.program_id(0)]
        lane = lax.broadcasted_iota(jnp.int32, (length, 128), 1) < HD
        g_context = dot_nt(ga[0], wo[...]).astype(BF)
        for p in range(width // 128):
            cols = slice(p*128,(p+1)*128)
            q2, k2, v2, c2 = q[0,:,cols], k[0,:,cols], v[0,:,cols], g_context[:,cols]
            both = [halves_of(a, lane) for a in (q2,k2,v2,c2)]
            gq = gk = gv = None
            for i in range(2):
                qh,kh,vh,ch = (b[i] for b in both)
                s = jnp.where(live, dot_nt(kh, q2) * SCALE, -1000000000.0)
                e = jnp.exp(s - jnp.max(s, axis=0, keepdims=True))
                pr = e / jnp.sum(e, axis=0, keepdims=True)
                gp = dot_nt(vh, c2)
                ds = (pr * (gp - jnp.sum(pr*gp, axis=0, keepdims=True))).astype(BF)
                a, b, c = dot(pr.astype(BF), ch), dot(ds, qh), dot(kh.T, ds)
                gv, gk, gq = (a, b, c) if gv is None else (gv+a, gk+b, gq+c)
            dq[0,:,cols] = (gq.T * SCALE).astype(BF)
            dk[0,:,cols] = (gk * SCALE).astype(BF)
            dv[0,:,cols] = gv.astype(BF)
        dx[0] = (gf[0] + dot_nt(dq[0], wqkv[0]) + dot_nt(dk[0], wqkv[1]) + dot_nt(dv[0], wqkv[2])).astype(BF)
        sums[0:1] += col_sum(dq[0].astype(F32))
        sums[1:2] += col_sum(dv[0].astype(F32))
    seq = pl.BlockSpec((1, length, width), lambda i, lens: (i, 0, 0))
    whole = lambda a: pl.BlockSpec(a.shape, lambda i, lens: (0,) * a.ndim, pipeline_mode=pl.Buffered(1))
    return pl.pallas_call(body, out_shape=[jax.ShapeDtypeStruct(q.shape, BF)]*4+[jax.ShapeDtypeStruct((8,width),F32)],
        grid_spec=pltpu.PrefetchScalarGridSpec(num_scalar_prefetch=1, grid=(n,), in_specs=[seq]*5+[whole(w_out),whole(w_qkv)], out_specs=[seq]*4+[pl.BlockSpec((8,width),lambda i,lens:(0,0))]),
        compiler_params=pltpu.CompilerParams(vmem_limit_bytes=50<<20))(lens, q, k, v, g_attn, g_first, w_out, w_qkv)

def project(dealt, w_qkv, bias):
    n, length, width = dealt.shape
    def body(x, w, b, q, k, v):
        for i,o in enumerate((q,k,v)):
            r = dot(x[0], w[i])
            if i != 1: r = r + b[i//2:i//2+1]
            o[0] = r.astype(BF)
    seq = pl.BlockSpec((1, length, width), lambda i: (i, 0, 0))
    whole = lambda a: pl.BlockSpec(a.shape, lambda i: (0,) * a.ndim, pipeline_mode=pl.Buffered(1))
    return pl.pallas_call(body, out_shape=[jax.ShapeDtypeStruct(dealt.shape,BF)]*3, grid=(n,), in_specs=[seq,whole(w_qkv),whole(bias)], out_specs=[seq]*3,
        compiler_params=pltpu.CompilerParams(vmem_limit_bytes=40<<20))(dealt, w_qkv, bias)


def weight_grad(left, right):
    return jnp.einsum("grf,grd->fd", left, right, preferred_element_type=F32).astype(BF)


def layer(position, dealt, seq_lens, cotangent, full):
    w_qkv, w_out, w_up, w_down, vectors, bias_up = full
    q, k, v = project(dealt, w_qkv, vectors[:2])
    context = attention_forward(seq_lens, q, k, v)
    layer_out, g_first, g_attn, hidden, g_hidden, mid_low, g_ffn, sums, g_bias_up = middle(
        position, context, dealt, cotangent, vectors, bias_up, w_out, w_up, w_down
    )
    g_down = weight_grad(hidden, g_ffn)
    g_up = weight_grad(mid_low, g_hidden)
    g_out = weight_grad(context, g_attn)
    g_input, g_q, g_k, g_v, sums_qv = attention_backward(
        seq_lens, q, k, v, g_attn, g_first, w_out, w_qkv
    )
    g_qkv = [weight_grad(dealt, g) for g in (g_q, g_k, g_v)]
    vectors = jnp.concatenate([sums_qv[:2], sums[2:]], axis=0)
    return layer_out, g_input, (g_qkv, g_out, g_up, g_down, vectors, g_bias_up)


SMALL = ("bias_q", "bias_v", "bias_out", "gain_one", "offset_one", "bias_down", "gain_two", "offset_two")


def pack_small(bias_qv, bias_out, gain_one, offset_one, bias_up, bias_down, gain_two, offset_two):
    return jnp.concatenate(
        [bias_qv[0], bias_qv[1], bias_out, gain_one, offset_one, bias_down, gain_two, offset_two, bias_up]
    )


def gather_weights(grid, place, shard, model_width, ff_width):
    (proj_qkv, bias_qv, proj_out, bias_out, gain_one, offset_one, proj_up, bias_up, proj_down, bias_down, gain_two, offset_two) = shard
    rows = proj_out.shape[0]
    chunks = ff_width // model_width
    small = pack_small(bias_qv, bias_out, gain_one, offset_one, bias_up, bias_down, gain_two, offset_two)
    small = jnp.pad(small[None, :], ((0, 7), (0, model_width - small.shape[0])))
    here = dict(HERE)
    first = join(
        [
            (proj_qkv[0], [("q", here, rows)]),
            (proj_qkv[1], [("k", here, rows)]),
            (small, [("s", here, 8)]),
        ]
    )
    second = join([(proj_qkv[2], [("v", here, rows)]), (proj_out, [("o", here, rows)])])
    one = gather_core(grid, gather_late_z(grid, first) + gather_early_z(grid, second))
    up = [
        (proj_up[:, t * model_width : (t + 1) * model_width], [(f"u{t}", here, rows)])
        for t in range(chunks)
    ]
    two = gather_core(
        grid,
        gather_late_z(grid, join(up[:2]))
        + gather_early_z(grid, join(up[2:] + [(proj_down, [("d", here, proj_down.shape[0])])])),
    )
    count = grid.fsdp * grid.size["y"] * 2
    weights = assemble(
        grid,
        place,
        one,
        {
            "q": (0, 0, 0),
            "k": (0, model_width, 0),
            "v": (0, 2 * model_width, 0),
            "o": (1, 0, 0),
            "s": (2, 0, 0),
        },
        [(3 * model_width, model_width), (model_width, model_width), (count * 8, model_width)],
    )
    ffn = assemble(
        grid,
        place,
        two,
        {"d": (1, 0, 0), **{f"u{t}": (0, 0, t * model_width) for t in range(chunks)}},
        [(model_width, ff_width), (ff_width, model_width)],
    )
    small = weights[2].reshape(count, 8, model_width)[:, 0, : 8 * rows + ff_width // count].astype(F32)
    vectors = small[:, : 8 * rows].reshape(count, 8, rows).transpose(1, 0, 2).reshape(8, model_width)
    bias_up = small[:, 8 * rows :].reshape(1, ff_width)
    w_qkv = weights[0].reshape(3, model_width, model_width)
    return w_qkv, weights[1], ffn[0], ffn[1], vectors, bias_up


def plain_weights(shard):
    axes = (1, 1, 0, 0, 0, 0, 0, 0, 0, 0, 0, 0)
    w = [lax.all_gather(w, AXES, axis=a, tiled=True) for w, a in zip(shard, axes)]
    vectors = jnp.stack([w[1][0], w[1][1], w[3], w[4], w[5], w[9], w[10], w[11]]).astype(F32)
    return w[0], w[2], w[6], w[8], vectors, w[7][None, :].astype(F32)


def plain_sums(grads):
    g_qkv, g_out, g_up, g_down, vectors, g_bias_up = grads

    def total(g, axis):
        return lax.psum_scatter(g.astype(F32), AXES, scatter_dimension=axis, tiled=True)

    vectors = total(vectors, 1)
    return (
        total(jnp.stack(g_qkv), 1),
        vectors[:2],
        total(g_out, 0),
        vectors[2],
        vectors[3],
        vectors[4],
        total(g_up, 0),
        total(g_bias_up[0], 0),
        total(g_down, 0),
        vectors[5],
        vectors[6],
        vectors[7],
    )


def reduce_gradients(grid, place, grads, rows):
    g_qkv, g_out, g_up, g_down, vectors, g_bias_up = grads
    model_width, ff_width = g_up.shape
    chunks = ff_width // model_width
    count = grid.fsdp * grid.size["y"] * 2
    ff_rows = ff_width // count
    plane = grid.size["x"] * grid.size["y"]

    ups = [(f"u{t}", rows) for t in range(chunks)]
    late = late_z_labels(grid, ups[:1], ups[1:2])
    early_a = early_z_labels(grid, "yx", ups[2:] )
    early_b = early_z_labels(grid, "xy", [("d", ff_rows)])
    made = spread(
        grid,
        place,
        [g_up, g_down],
        {"d": (1, 0), **{f"u{t}": (0, t * model_width) for t in range(chunks)}},
        late + early_a + early_b,
    )
    late, early_a, early_b = (add_core(grid, made[i : i + 2]) for i in (0, 2, 4))
    owned = {}

    def keep(bundle):
        at = 0
        for mat, _, n in bundle[1]:
            owned[mat] = bundle[0][at : at + n]
            at += n

    for b in reduce_late_z(grid, late, plane):
        keep(b)
    keep(reduce_early_z(grid, early_a, early_b))

    small = jnp.concatenate(
        [
            vectors.reshape(8, count, rows).transpose(1, 0, 2).reshape(count, 8 * rows),
            g_bias_up.reshape(count, ff_rows),
        ],
        axis=1,
    )
    small = jnp.pad(small[:, None, :], ((0, 0), (0, 7), (0, model_width - small.shape[1])))
    small = small.reshape(count * 8, model_width).astype(BF)
    late = late_z_labels(grid, [("q", rows)], [("k", rows), ("s", 8)])
    early_a = early_z_labels(grid, "yx", [("v", rows)])
    early_b = early_z_labels(grid, "xy", [("o", rows)])
    made = spread(
        grid,
        place,
        [*g_qkv, g_out, small],
        {"q": (0, 0), "k": (1, 0), "v": (2, 0), "o": (3, 0), "s": (4, 0)},
        late + early_a + early_b,
    )
    late, early_a, early_b = (add_core(grid, made[i : i + 2]) for i in (0, 2, 4))
    for b in reduce_late_z(grid, late, plane):
        keep(b)
    keep(reduce_early_z(grid, early_a, early_b))
    small = owned["s"][0]
    named = {name: small[i * rows : (i + 1) * rows] for i, name in enumerate(SMALL)}
    return (
        jnp.stack([owned["q"], owned["k"], owned["v"]]),
        jnp.stack([named["bias_q"], named["bias_v"]]),
        owned["o"],
        named["bias_out"],
        named["gain_one"],
        named["offset_one"],
        jnp.concatenate([owned[f"u{t}"] for t in range(chunks)], axis=1),
        small[8 * rows : 8 * rows + ff_rows],
        owned["d"],
        named["bias_down"],
        named["gain_two"],
        named["offset_two"],
    )


def deal_by_pairs(inputs, dealing, dp_count, fsdp_count, dp_index, fsdp_index):
    slots = inputs.shape[0]
    per_peer = fsdp_count * slots
    mine = (dp_index * fsdp_count + fsdp_index) * slots
    slot_range = jnp.arange(slots, dtype=jnp.int32)
    distance = slot_range[:, None] ^ dp_index
    sources = lax.dynamic_slice_in_dim(dealing, mine, slots)
    hit = (sources // per_peer)[None, :] == distance
    position = jnp.sum(jnp.where(hit, slot_range[None, :], 0), axis=1)
    came_from = jnp.sum(jnp.where(hit, sources[None, :], 0), axis=1)
    table = dealing.reshape(dp_count, fsdp_count, slots)
    table = lax.dynamic_index_in_dim(table, fsdp_index, 1, keepdims=False)
    own = jnp.where((table >= mine) & (table < mine + slots), table - mine, 0)
    own = jnp.sum(own, axis=1)
    slot = jnp.sum(jnp.where(jnp.arange(dp_count, dtype=jnp.int32)[None, :] == distance, own[None, :], 0), axis=1)
    return slot, position, came_from


def swap(array, k, dp_count, fsdp_count):
    if k == 0:
        return array
    pairs = [
        (d * fsdp_count + f, (d ^ k) * fsdp_count + f)
        for d in range(dp_count)
        for f in range(fsdp_count)
    ]
    return lax.ppermute(array, AXES, pairs)


def shards(inputs, dealing, lengths, *rest):
    weights, cotangent = rest[:-1], rest[-1]
    slots, length, model_width = inputs.shape
    ff_width = weights[6].shape[1]
    dp_count, fsdp_count = lax.axis_size("dp"), lax.axis_size("fsdp")
    dp_index, fsdp_index = lax.axis_index("dp"), lax.axis_index("fsdp")
    rows = weights[2].shape[0]
    by_blocks = rows % 8 == 0 and fsdp_count == 2 * NZ and dp_count == 4
    if by_blocks:
        grid = Grid(dp_count, fsdp_count)
        nx = grid.size["x"]
        place = jnp.stack([dp_index // 2, dp_index % 2, fsdp_index // nx, fsdp_index % nx])
        full = gather_weights(grid, place, weights, model_width, ff_width)
    else:
        full = plain_weights(weights)
    if dp_count == slots:
        slot, position, came_from = deal_by_pairs(
            inputs, dealing, dp_count, fsdp_count, dp_index, fsdp_index
        )
        dealt = jnp.stack(
            [
                swap(lax.dynamic_index_in_dim(inputs, slot[k], 0, keepdims=False), k, dp_count, fsdp_count)
                for k in range(slots)
            ]
        )
        seq_lens = jnp.take(lengths, came_from)
        layer_out, grad_rows, grads = layer(position, dealt, seq_lens, cotangent, full)
        input_grad = jnp.zeros_like(grad_rows)
        for k in range(slots):
            back = swap(grad_rows[k], k, dp_count, fsdp_count)
            input_grad = lax.dynamic_update_index_in_dim(input_grad, back, slot[k], 0)
    else:
        mine = (dp_index * fsdp_count + fsdp_index) * slots
        slot_range = jnp.arange(slots, dtype=jnp.int32)
        peers = jnp.arange(dp_count, dtype=jnp.int32)
        sources = lax.dynamic_slice_in_dim(dealing, mine, slots)
        take = ((sources // slots // fsdp_count)[:, None] == peers[None, :]).astype(BF)
        wanted = lax.dynamic_index_in_dim(
            dealing.reshape(dp_count, fsdp_count, slots), fsdp_index, 1, keepdims=False
        )
        send = jnp.sum(
            (wanted[:, :, None] == (mine + slot_range)[None, None, :]).astype(jnp.int32), axis=1
        ).astype(BF)
        outgoing = jnp.einsum("em,mld->eld", send, inputs, preferred_element_type=F32).astype(BF)
        arrived = lax.all_to_all(outgoing, "dp", split_axis=0, concat_axis=0, tiled=True)
        dealt = jnp.einsum("ke,eld->kld", take, arrived, preferred_element_type=F32).astype(BF)
        layer_out, grad_rows, grads = layer(
            slot_range, dealt, jnp.take(lengths, sources), cotangent, full
        )
        returning = jnp.einsum("ke,kld->eld", take, grad_rows, preferred_element_type=F32).astype(BF)
        returned = lax.all_to_all(returning, "dp", split_axis=0, concat_axis=0, tiled=True)
        input_grad = jnp.einsum("em,eld->mld", send, returned, preferred_element_type=F32).astype(BF)
    if by_blocks:
        sums = reduce_gradients(grid, place, grads, rows)
    else:
        sums = plain_sums(grads)
    return (layer_out, input_grad, *sums)


def solution(mesh):
    return jax.shard_map(
        shards,
        mesh=mesh,
        in_specs=(
            P(("dp", "fsdp"), None, None),
            P(),
            P(),
            P(None, ("dp", "fsdp"), None),
            P(None, ("dp", "fsdp")),
            P(("dp", "fsdp"), None),
            P(("dp", "fsdp")),
            P(("dp", "fsdp")),
            P(("dp", "fsdp")),
            P(("dp", "fsdp"), None),
            P(("dp", "fsdp")),
            P(("dp", "fsdp"), None),
            P(("dp", "fsdp")),
            P(("dp", "fsdp")),
            P(("dp", "fsdp")),
            P(("dp", "fsdp"), None, None),
        ),
        out_specs=(
            P(("dp", "fsdp"), None, None),
            P(("dp", "fsdp"), None, None),
            P(None, ("dp", "fsdp"), None),
            P(None, ("dp", "fsdp")),
            P(("dp", "fsdp"), None),
            P(("dp", "fsdp")),
            P(("dp", "fsdp")),
            P(("dp", "fsdp")),
            P(("dp", "fsdp"), None),
            P(("dp", "fsdp")),
            P(("dp", "fsdp"), None),
            P(("dp", "fsdp")),
            P(("dp", "fsdp")),
            P(("dp", "fsdp")),
        ),
        check_vma=False,
    )
```
